32 devices in a mesh: expert: 8 (over y, x, core), tensor: 4 (over z).
Axes of the slice: x: 2, y: 2, z: 4, core: 2. Of those that a mesh axis runs over, the one named last changes fastest.
Arguments:
- tokens: bfloat16 [2560, 4096], P('expert', 'tensor'), may hold values from -6 to 6
- grad_out: bfloat16 [2560, 4096], P('expert', 'tensor'), may hold values from -6 to 6
- routes: int32 [2560, 4], P('expert'), may hold values from 0 to 7, all different within a row; in each aligned block of 320 rows (0 to 319, 320 to 639, ...) at most 200 rows name the same one
- route_weights: float32 [2560, 4], P('expert'), may hold values from 0.05 to 0.5
- swap_flags: int32 [4], replicated, may hold values from 0 to 1023
- weights: bfloat16 [8, 3, 1536, 4096], P('expert', None, None, 'tensor'), may hold values from -0.09375 to 0.09375
- first_moment: bfloat16 [8, 3, 1536, 4096], P('expert', None, None, 'tensor'), may hold values from -8 to 8
- second_moment: bfloat16 [8, 3, 1536, 4096], P('expert', None, None, 'tensor'), may hold values from 1 to 30
Outputs:
- combined: bfloat16 [2560, 4096], P('expert', 'tensor')
- update: bfloat16 [8, 3, 1536, 4096], P('expert', None, None, 'tensor')
The draws below stay inside these ranges and needn't reach their ends.
Inputs may be any that keep to these rules, and one draw needn't show every extreme that they name: `routes`: in each aligned block of 320 rows no expert is named by more than 200 rows, a bound that some block reaches; a row names 4 different experts.
All inputs are finite; a program needn't handle non-finite values.
Results may differ from the reference program's by a relative error of at most 0.023.
Values may be sent and summed in bfloat16 or wider, within the bound.
A program may use at most 192 MiB of HBM per device.

```python
import math
import jax
import jax.numpy as jnp
import numpy as np
from jax import lax

D = 4096
FF = 1536
TOK_DEV = 320
ROUTES = 4
EXPERTS = 8
TOKENS = 2560
CAP = 200
D_SHARD = 1024
N_EXPERT = 8
N_TENSOR = 4


def set_ends(values, stream_key, low, top_value):
    extent = values.shape
    place = [jax.random.randint(jax.random.fold_in(stream_key, axis), (), 0, extent[axis]) for axis in range(len(extent))]
    values = values.at[tuple(place)].set(low)
    longest = extent.index(max(extent))
    place[longest] = (place[longest] + 1) % extent[longest]
    return values.at[tuple(place)].set(top_value)


def block_scale(key, extent, split, least, top_value):
    factor_of = 1.0
    for position, blocks in split:
        draws = jax.random.uniform(jax.random.fold_in(jax.random.fold_in(key, 6), position), (blocks,), jnp.float32, least / len(split), top_value / len(split))
        factor_of = factor_of * jnp.repeat(jnp.exp(draws), extent[position] // blocks).reshape((-1,) + (1,) * (len(extent) - 1 - position))
    return factor_of


def deal_out(rng, own, number, rows, count, top, reach, skew):
    order = jax.random.permutation(rng, count)
    heavy_load, common = load_shares(count, rows * top, reach, skew, True), load_shares(count, rows * top, reach, skew, False)
    places = jnp.arange(count)

    def named(lengths, turn):
        used = int((lengths > 0).sum())
        fixed = max(1, used // 4)
        passed = fixed + (places - fixed + turn * (used - fixed)) % max(1, count - fixed)
        return jnp.zeros((count,), jnp.int32).at[order[jnp.where(places < fixed, places, passed)]].set(jnp.asarray(lengths, jnp.int32))

    lengths = jnp.where(number % 4 == 0, named(heavy_load, number // 4), named(common, number - number // 4 - 1))
    mixed = jax.random.permutation(jax.random.fold_in(own, 3), count)
    giver, taker = mixed[0:count // 2 * 2:2], mixed[1:count // 2 * 2:2]
    margin = jnp.minimum(lengths[giver] - 1, reach - lengths[taker]) // 2
    margin = jnp.where((giver == order[0]) | (taker == order[0]) | (lengths[taker] == 0), 0, jnp.maximum(margin, 0))
    passed = jax.random.randint(jax.random.fold_in(own, 4), (count // 2,), 0, 1 << 20) % (margin + 1)
    lengths = lengths.at[giver].add(-passed).at[taker].add(passed)
    labels = jnp.searchsorted(jnp.cumsum(lengths), jnp.arange(rows * top), side="right").astype(jnp.int32)
    table = labels.reshape(top, rows).T
    table = table[jax.random.permutation(jax.random.fold_in(own, 1), rows)]
    turn = jax.random.randint(jax.random.fold_in(own, 2), (rows, 1), 0, top)
    return jnp.take_along_axis(table, (jnp.arange(top)[None, :] + turn) % top, axis=1)


def load_shares(number_of, total, most, lean, full):
    loads = [(1 << 20) // math.isqrt(standing ** lean) + 1 for standing in range(1, number_of + 1)]
    largest = most if full else min(most, max(-(-total // number_of), total * loads[0] // sum(loads)))
    least = 1 if total - largest >= number_of - 1 else 0
    holding, spare = [largest] + [least] * (number_of - 1), total - largest - least * (number_of - 1)
    while spare > 0:
        movable = [i for i in range(1, number_of) if holding[i] < largest] or [i for i in range(1, number_of) if holding[i] < most]
        mass, remaining = sum([loads[i] for i in movable]), spare
        for i in movable:
            addition = min(most - holding[i], max(1, remaining * loads[i] // mass), spare)
            holding[i] = holding[i] + addition
            spare = spare - addition
    return np.array(holding)


def bell_draw(stream_key, shape, width, limit, cuts=(), kind=jnp.bfloat16):
    entries = jax.random.normal(stream_key, shape, jnp.float32) * width
    if len(cuts) > 0:
        entries = block_scale(stream_key, shape, cuts, -0.22, 0.18) * entries
    return jnp.clip(entries, min=-limit, max=limit).astype(kind)


def setup_inputs(seed: int = 0) -> dict:
    keys = jax.random.split(jax.random.key(seed), 9)
    tokens = bell_draw(keys[0], (TOKENS, D), 1.0, 6.0, ((0, 8), (1, 4)))
    grad_out = bell_draw(keys[1], (TOKENS, D), 1.0, 6.0, ((0, 8), (1, 4)))
    routes_keys = jax.random.split(jax.random.fold_in(keys[2], 1), TOKENS // TOK_DEV)
    routes_turns = jax.random.permutation(jax.random.fold_in(keys[2], 3), TOKENS // TOK_DEV)
    routes = jax.vmap(lambda own, number: deal_out(jax.random.fold_in(keys[2], 2), own, number, TOK_DEV, EXPERTS, ROUTES, CAP, 2))(routes_keys, routes_turns).reshape((TOKENS, ROUTES))
    route_weights = jnp.clip(jnp.exp(math.log(0.5) - 2.3025851 * jax.random.uniform(keys[3], (TOKENS, ROUTES), jnp.float32) ** block_scale(keys[3], (TOKENS, ROUTES), ((0, 8),), -0.2, 0.2)), 0.05, 0.5)
    swap_flags = set_ends(jax.random.randint(keys[4], (EXPERTS // 2,), 0, 1024), jax.random.fold_in(keys[4], 1), 0, 1023).astype(jnp.int32)
    weights = bell_draw(keys[5], (EXPERTS, 3, FF, D), D ** -0.5, 0.09375, ((0, 8), (3, 4)))
    first_moment = bell_draw(keys[6], (EXPERTS, 3, FF, D), 2.0, 8.0, ((0, 8), (3, 4)))
    second_moment = jnp.clip(jnp.exp(math.log(30.0) - 3.4011974 * jax.random.uniform(keys[7], (EXPERTS, 3, FF, D), jnp.float32) ** block_scale(keys[7], (EXPERTS, 3, FF, D), ((0, 8), (3, 4)), -0.2, 0.2)), 1.0, 30.0).astype(jnp.bfloat16)
    return {"tokens": tokens, "grad_out": grad_out, "routes": routes, "route_weights": route_weights, "swap_flags": swap_flags, "weights": weights, "first_moment": first_moment, "second_moment": second_moment}


correction_one = 1.0 - 0.9 ** 20
correction_two = 1.0 - 0.95 ** 20

def block_sum(left_rows, right_rows):
    left_blocks = left_rows.reshape(left_rows.shape[0], N_TENSOR, D_SHARD).astype(jnp.float32)
    right_blocks = right_rows.reshape(right_rows.shape[0], N_TENSOR, D_SHARD).astype(jnp.float32)
    partials = jnp.einsum('sjd,rjd->jsr', left_blocks, right_blocks)
    rounded = lax.optimization_barrier(partials.astype(jnp.bfloat16))
    return lax.optimization_barrier(jnp.sum(rounded.astype(jnp.float32), axis=0))

def reference(tokens, grad_out, routes, route_weights, swap_flags, weights, first_moment, second_moment):
    block_slots = TOK_DEV * ROUTES
    slot_total = TOKENS * ROUTES
    experts_range = jnp.arange(EXPERTS, dtype=jnp.int32)
    flat_ids = routes.reshape(N_EXPERT, block_slots).astype(jnp.int32)
    id_onehot = (flat_ids[:, :, None] == experts_range[None, None, :]).astype(jnp.int32)
    slot_rank = lax.optimization_barrier(jnp.sum((jnp.cumsum(id_onehot, axis=1) - id_onehot) * id_onehot, axis=2))
    group_index = jnp.arange(N_EXPERT, dtype=jnp.int32)[:, None]
    slot_index = (flat_ids * (N_EXPERT * CAP) + group_index * CAP + slot_rank).reshape(-1)
    flat_slot = jnp.arange(slot_total, dtype=jnp.int32)
    table_rows = jnp.full((EXPERTS * N_EXPERT * CAP,), slot_total, jnp.int32).at[slot_index].set(flat_slot)
    table_rows = table_rows.reshape(EXPERTS, N_EXPERT * CAP)
    token_pad = jnp.concatenate([tokens, jnp.zeros((1, D), tokens.dtype)], axis=0)
    scaled_grad = (route_weights[:, :, None] * grad_out[:, None, :].astype(jnp.float32)).astype(jnp.bfloat16)
    grad_pad = jnp.concatenate([scaled_grad.reshape(slot_total, D), jnp.zeros((1, D), jnp.bfloat16)], axis=0)

    def expert_pass(packed):
        entry_rows, expert_weight, moment_one, moment_two = packed
        token_slots = token_pad[entry_rows // ROUTES]
        grad_slots = grad_pad[entry_rows]
        preact = block_sum(token_slots, expert_weight[0:2].reshape(2 * FF, D))
        gate_pre = preact[:, :FF]
        up_pre = preact[:, FF:]
        sig_gate = jax.nn.sigmoid(gate_pre)
        hidden = (gate_pre * sig_gate * up_pre).astype(jnp.bfloat16)
        output_slots = jnp.dot(hidden, expert_weight[2], preferred_element_type=jnp.float32).astype(jnp.bfloat16)
        hidden_grad = block_sum(grad_slots, expert_weight[2])
        gate_grad = (hidden_grad * up_pre * sig_gate * (1.0 + gate_pre * (1.0 - sig_gate))).astype(jnp.bfloat16)
        up_grad = (hidden_grad * gate_pre * sig_gate).astype(jnp.bfloat16)
        weight_grad = jnp.stack([jnp.dot(gate_grad.T, token_slots, preferred_element_type=jnp.float32), jnp.dot(up_grad.T, token_slots, preferred_element_type=jnp.float32), jnp.dot(hidden.T, grad_slots, preferred_element_type=jnp.float32)])
        moment_new = 0.9 * moment_one.astype(jnp.float32) + 0.1 * weight_grad
        square_new = 0.95 * moment_two.astype(jnp.float32) + 0.05 * weight_grad * weight_grad
        step_dir = moment_new / correction_one / (jnp.sqrt(square_new / correction_two) + 1e-08)
        return (step_dir.astype(jnp.bfloat16), output_slots)
    step_all, output_all = lax.map(expert_pass, (table_rows, weights, first_moment, second_moment))
    gathered_out = output_all.reshape(EXPERTS * N_EXPERT * CAP, D)[slot_index]
    gathered_out = gathered_out.reshape(TOKENS, ROUTES, D).astype(jnp.float32)
    combined = lax.optimization_barrier(jnp.sum(route_weights[:, :, None] * gathered_out, axis=1)).astype(jnp.bfloat16)
    paired = jnp.repeat(jnp.bitwise_and(swap_flags.astype(jnp.int32), 1), 2)
    held_expert = jnp.where(paired == 1, jnp.bitwise_xor(experts_range, 1), experts_range)
    update = jnp.take(step_all, held_expert, axis=0)
    return (combined, update)
```

```python
import jax
import jax.numpy as jnp
from jax import lax
from jax.sharding import PartitionSpec as P


correction_one = 1.0 - 0.9**20
correction_two = 1.0 - 0.95**20
PAIR = 128
BLOCK = 256


def contract_last(left_rows, right_rows):
    return lax.dot_general(
        left_rows, right_rows, (((1,), (1,)), ((), ())), preferred_element_type=jnp.float32
    )


def contract_first(left_rows, right_rows):
    return lax.dot_general(
        left_rows, right_rows, (((0,), (0,)), ((), ())), preferred_element_type=jnp.float32
    )


def line_sum(part):
    count = lax.axis_size("tensor")
    half = count // 2
    spot = lax.axis_index("tensor")
    total = part
    for step in range(half - 1):
        pairs = [(step, step + 1), (count - 1 - step, count - 2 - step)]
        total = total + lax.ppermute(total, "tensor", pairs)
    total = total + lax.ppermute(total, "tensor", [(half - 1, half), (half, half - 1)])
    for step in range(half - 2, -1, -1):
        pairs = [(step + 1, step), (count - 2 - step, count - 1 - step)]
        came = lax.ppermute(total, "tensor", pairs)
        total = jnp.where((spot == step) | (spot == count - 1 - step), came, total)
    return total


def adam(moment, square, grad):
    moment_new = 0.9 * moment.astype(jnp.float32) + 0.1 * grad
    square_new = 0.95 * square.astype(jnp.float32) + 0.05 * grad * grad
    step = moment_new / correction_one / (jnp.sqrt(square_new / correction_two) + 1e-08)
    return step.astype(jnp.bfloat16)


def body(tokens, grad_out, routes, route_weights, swap_flags, weights, first_moment, second_moment):
    expert_count = lax.axis_size("expert")
    tok_count, route_count = routes.shape
    feat_width = tokens.shape[1]
    slot_cap = tok_count * route_count * 5 // (4 * expert_count)
    slot_total = tok_count * route_count
    slot_rows = expert_count * slot_cap
    positions = jnp.arange(expert_count, dtype=jnp.int32)
    paired = jnp.repeat(jnp.bitwise_and(swap_flags, 1), 2)
    traded = jnp.sum(jnp.where(positions == lax.axis_index("expert"), paired, 0)) == 1

    onehot = (routes.reshape(-1)[:, None] == positions[None, :]).astype(jnp.int32)
    slot_rank = jnp.sum((jnp.cumsum(onehot, axis=0) - onehot) * onehot, axis=1)
    slot_index = routes * slot_cap + slot_rank.reshape(tok_count, route_count)
    slots = jnp.arange(slot_rows, dtype=jnp.int32)
    pick = jnp.zeros((slot_rows, tok_count), jnp.float32)
    pick_weight = jnp.zeros((slot_rows, tok_count), jnp.float32)
    for r in range(route_count):
        hit = slots[:, None] == slot_index[:, r][None, :]
        pick = pick + jnp.where(hit, 1.0, 0.0)
        pick_weight = pick_weight + jnp.where(hit, route_weights[:, r][None, :], 0.0)
    pick = pick.astype(jnp.bfloat16)
    slot_weight = jnp.sum(pick_weight, axis=1)
    pick_weight = pick_weight.astype(jnp.bfloat16)

    def dispatch(rows):
        return lax.all_to_all(
            rows.reshape(expert_count, slot_cap, feat_width), "expert", 0, 0, tiled=True
        ).reshape(slot_rows, feat_width)

    send_tokens = jnp.dot(pick, tokens, preferred_element_type=jnp.float32).astype(jnp.bfloat16)
    token_slots = dispatch(send_tokens)
    send_grads = (
        slot_weight[:, None] * jnp.dot(pick, grad_out, preferred_element_type=jnp.float32)
    ).astype(jnp.bfloat16)
    grad_slots = dispatch(send_grads)

    gate_w, up_w, down_w = weights[0, 0], weights[0, 1], weights[0, 2]
    hidden_width = gate_w.shape[0]
    gates, ups, hiddens = [], [], []
    for c in range(0, hidden_width, PAIR):
        rows = jnp.concatenate([gate_w[c : c + PAIR], up_w[c : c + PAIR]], axis=0)
        both = line_sum(contract_last(token_slots, rows).astype(jnp.bfloat16)).astype(jnp.float32)
        gate_pre, up_pre = both[:, :PAIR], both[:, PAIR:]
        gates.append(gate_pre)
        ups.append(up_pre)
        hiddens.append((gate_pre * jax.nn.sigmoid(gate_pre) * up_pre).astype(jnp.bfloat16))
    hidden = jnp.concatenate(hiddens, axis=1)
    output_slots = jnp.dot(hidden, down_w, preferred_element_type=jnp.float32).astype(jnp.bfloat16)
    returned = dispatch(output_slots)
    combined = contract_first(pick_weight, returned).astype(jnp.bfloat16)

    def settle(which, c, left, right):
        grad = contract_first(left, right)
        span = slice(c, c + BLOCK)
        own = adam(first_moment[0, which, span], second_moment[0, which, span], grad)
        moved = lax.ppermute(own, "expert", [(i, i ^ 1) for i in range(expert_count)])
        return jnp.where(traded, moved, own)

    gate_steps, up_steps, down_steps = [], [], []
    for c in range(0, hidden_width, BLOCK):
        span = range(c // PAIR, (c + BLOCK) // PAIR)
        hidden_grad = line_sum(
            contract_last(grad_slots, down_w[c : c + BLOCK]).astype(jnp.bfloat16)
        ).astype(jnp.float32)
        gate_pre = jnp.concatenate([gates[k] for k in span], axis=1)
        up_pre = jnp.concatenate([ups[k] for k in span], axis=1)
        sig_gate = jax.nn.sigmoid(gate_pre)
        gate_grad = (hidden_grad * up_pre * sig_gate * (1.0 + gate_pre * (1.0 - sig_gate))).astype(
            jnp.bfloat16
        )
        up_grad = (hidden_grad * gate_pre * sig_gate).astype(jnp.bfloat16)
        down_steps.append(settle(2, c, hidden[:, c : c + BLOCK], grad_slots))
        gate_steps.append(settle(0, c, gate_grad, token_slots))
        up_steps.append(settle(1, c, up_grad, token_slots))
    update = jnp.concatenate(gate_steps + up_steps + down_steps, axis=0)
    return combined, update.reshape(weights.shape)


def solution(mesh):
    placed = (
        P("expert", "tensor"),
        P("expert", "tensor"),
        P("expert", None),
        P("expert", None),
        P(),
        P("expert", None, None, "tensor"),
        P("expert", None, None, "tensor"),
        P("expert", None, None, "tensor"),
    )
    return jax.shard_map(
        body,
        mesh=mesh,
        in_specs=placed,
        out_specs=(P("expert", "tensor"), P("expert", None, None, "tensor")),
        check_vma=False,
    )
```

```python
import jax
import jax.numpy as jnp
from jax import lax
from jax.sharding import PartitionSpec as P


correction_one = 1.0 - 0.9**20
correction_two = 1.0 - 0.95**20
PAIR = 128
BLOCK = 256


def contract_last(left_rows, right_rows):
    return lax.dot_general(
        left_rows, right_rows, (((1,), (1,)), ((), ())), preferred_element_type=jnp.float32
    )


def contract_first(left_rows, right_rows):
    return lax.dot_general(
        left_rows, right_rows, (((0,), (0,)), ((), ())), preferred_element_type=jnp.float32
    )


def after(value, *earlier):
    return lax.optimization_barrier((value, *earlier))[0]


class LineSum:

    def __init__(self):
        count = lax.axis_size("tensor")
        half = count // 2
        self.count, self.half = count, half
        self.spot = lax.axis_index("tensor")
        self.hops = [[(k, k + 1), (count - 1 - k, count - 2 - k)] for k in range(half - 1)]
        self.hops.append([(half - 1, half), (half, half - 1)])
        self.hops += [
            [(k + 1, k), (count - 2 - k, count - 1 - k)] for k in range(half - 2, -1, -1)
        ]
        self.arrived = [[] for _ in self.hops]

    def add(self, part):
        total = part
        number = len(self.arrived[0])
        for h, pairs in enumerate(self.hops):
            waits = []
            for later in range(h, len(self.hops)):
                back = number - 2 - (later - h)
                if back >= 0:
                    waits.append(self.arrived[later][back])
            came = lax.ppermute(after(total, *waits), "tensor", pairs)
            self.arrived[h].append(came)
            if h < self.half:
                total = total + came
            else:
                low = 2 * self.half - 2 - h
                edge = (self.spot == low) | (self.spot == self.count - 1 - low)
                total = jnp.where(edge, came, total)
        return total


def adam(moment, square, grad):
    moment_new = 0.9 * moment.astype(jnp.float32) + 0.1 * grad
    square_new = 0.95 * square.astype(jnp.float32) + 0.05 * grad * grad
    step = moment_new / correction_one / (jnp.sqrt(square_new / correction_two) + 1e-08)
    return step.astype(jnp.bfloat16)


def body(tokens, grad_out, routes, route_weights, swap_flags, weights, first_moment, second_moment):
    expert_count = lax.axis_size("expert")
    tok_count, route_count = routes.shape
    feat_width = tokens.shape[1]
    slot_cap = tok_count * route_count * 5 // (4 * expert_count)
    slot_total = tok_count * route_count
    slot_rows = expert_count * slot_cap
    positions = jnp.arange(expert_count, dtype=jnp.int32)
    paired = jnp.repeat(jnp.bitwise_and(swap_flags, 1), 2)
    traded = jnp.sum(jnp.where(positions == lax.axis_index("expert"), paired, 0)) == 1

    onehot = (routes.reshape(-1)[:, None] == positions[None, :]).astype(jnp.int32)
    slot_rank = jnp.sum((jnp.cumsum(onehot, axis=0) - onehot) * onehot, axis=1)
    slot_index = routes * slot_cap + slot_rank.reshape(tok_count, route_count)
    slots = jnp.arange(slot_rows, dtype=jnp.int32)
    pick = jnp.zeros((slot_rows, tok_count), jnp.float32)
    pick_weight = jnp.zeros((slot_rows, tok_count), jnp.float32)
    for r in range(route_count):
        hit = slots[:, None] == slot_index[:, r][None, :]
        pick = pick + jnp.where(hit, 1.0, 0.0)
        pick_weight = pick_weight + jnp.where(hit, route_weights[:, r][None, :], 0.0)
    pick = pick.astype(jnp.bfloat16)
    slot_weight = jnp.sum(pick_weight, axis=1)
    pick_weight = pick_weight.astype(jnp.bfloat16)

    def dispatch(rows):
        return lax.all_to_all(
            rows.reshape(expert_count, slot_cap, feat_width), "expert", 0, 0, tiled=True
        ).reshape(slot_rows, feat_width)

    send_tokens = jnp.dot(pick, tokens, preferred_element_type=jnp.float32).astype(jnp.bfloat16)
    token_slots = dispatch(send_tokens)
    send_grads = (
        slot_weight[:, None] * jnp.dot(pick, grad_out, preferred_element_type=jnp.float32)
    ).astype(jnp.bfloat16)
    grad_slots = dispatch(send_grads)

    hidden_width = weights.shape[2]
    gate_up_w, down_w = weights[0, 0:2], weights[0, 2]
    line = LineSum()
    gates, ups, hiddens = [], [], []

    def forward(c):
        rows = gate_up_w[:, c : c + PAIR].reshape(2 * PAIR, feat_width)
        both = line.add(contract_last(token_slots, rows).astype(jnp.bfloat16)).astype(jnp.float32)
        gate_pre, up_pre = both[:, :PAIR], both[:, PAIR:]
        gates.append(gate_pre)
        ups.append(up_pre)
        hiddens.append((gate_pre * jax.nn.sigmoid(gate_pre) * up_pre).astype(jnp.bfloat16))

    def settle(first, second, left, right):
        own = adam(first, second, contract_first(left, right))
        moved = lax.ppermute(own, "expert", [(i, i ^ 1) for i in range(expert_count)])
        return jnp.where(traded, moved, own)

    gate_up_steps, down_steps = [], []

    def backward(c):
        hidden_grad = line.add(
            contract_last(grad_slots, down_w[c : c + BLOCK]).astype(jnp.bfloat16)
        ).astype(jnp.float32)
        span = slice(c // PAIR, (c + BLOCK) // PAIR)
        gate_pre = jnp.concatenate(gates[span], axis=1)
        up_pre = jnp.concatenate(ups[span], axis=1)
        sig_gate = jax.nn.sigmoid(gate_pre)
        gate_grad = (hidden_grad * up_pre * sig_gate * (1.0 + gate_pre * (1.0 - sig_gate))).astype(
            jnp.bfloat16
        )
        up_grad = (hidden_grad * gate_pre * sig_gate).astype(jnp.bfloat16)
        own = (2 * BLOCK, feat_width)
        gate_up_steps.append(
            settle(
                first_moment[0, 0:2, c : c + BLOCK].reshape(own),
                second_moment[0, 0:2, c : c + BLOCK].reshape(own),
                jnp.concatenate([gate_grad, up_grad], axis=1),
                token_slots,
            ).reshape(2, BLOCK, feat_width)
        )

    def down(c):
        rows = slice(c, c + 2 * BLOCK)
        left = jnp.concatenate(hiddens[c // PAIR : (c + 2 * BLOCK) // PAIR], axis=1)
        down_steps.append(settle(first_moment[0, 2, rows], second_moment[0, 2, rows], left, grad_slots))

    blocks = list(range(0, hidden_width, BLOCK))
    for number, c in enumerate(blocks):
        forward(c)
        forward(c + PAIR)
        if number % 2 == 1:
            down(blocks[number - 1])
        if number < len(blocks) - 2:
            backward(c)
    hidden = jnp.concatenate(hiddens, axis=1)
    output_slots = jnp.dot(
        hidden, down_w, preferred_element_type=jnp.float32
    ).astype(jnp.bfloat16)
    returned = dispatch(output_slots)
    combined = contract_first(pick_weight, returned).astype(jnp.bfloat16)
    for c in blocks[-2:]:
        backward(c)
    update = jnp.concatenate(
        [jnp.concatenate(gate_up_steps, axis=1), jnp.concatenate(down_steps, axis=0)[None]], axis=0
    )
    return combined, update[None]


def solution(mesh):
    placed = (
        P("expert", "tensor"),
        P("expert", "tensor"),
        P("expert", None),
        P("expert", None),
        P(),
        P("expert", None, None, "tensor"),
        P("expert", None, None, "tensor"),
        P("expert", None, None, "tensor"),
    )
    return jax.shard_map(
        body,
        mesh=mesh,
        in_specs=placed,
        out_specs=(P("expert", "tensor"), P("expert", None, None, "tensor")),
        check_vma=False,
    )
```

```python
import jax
import jax.numpy as jnp
from jax import lax
from jax.sharding import PartitionSpec as P


correction_one = 1.0 - 0.9**20
correction_two = 1.0 - 0.95**20
PAIR = 128
BLOCK = 256
WINDOW = 2
LAG = 1


def contract_last(left_rows, right_rows):
    return lax.dot_general(
        left_rows, right_rows, (((1,), (1,)), ((), ())), preferred_element_type=jnp.float32
    )


def contract_first(left_rows, right_rows):
    return lax.dot_general(
        left_rows, right_rows, (((0,), (0,)), ((), ())), preferred_element_type=jnp.float32
    )


def after(value, *earlier):
    return lax.optimization_barrier((value, *earlier))[0]


class LineSum:

    def __init__(self):
        count = lax.axis_size("tensor")
        half = count // 2
        self.count, self.half = count, half
        self.spot = lax.axis_index("tensor")
        self.hops = [[(k, k + 1), (count - 1 - k, count - 2 - k)] for k in range(half - 1)]
        self.hops.append([(half - 1, half), (half, half - 1)])
        self.hops += [
            [(k + 1, k), (count - 2 - k, count - 1 - k)] for k in range(half - 2, -1, -1)
        ]
        self.arrived = [[] for _ in self.hops]

    def add(self, part):
        total = part
        number = len(self.arrived[0])
        for h, pairs in enumerate(self.hops):
            waits = []
            for later in range(h, len(self.hops)):
                back = number - WINDOW - LAG * (later - h)
                if back >= 0:
                    waits.append(self.arrived[later][back])
            came = lax.ppermute(after(total, *waits), "tensor", pairs)
            self.arrived[h].append(came)
            if h < self.half:
                total = total + came
            else:
                low = 2 * self.half - 2 - h
                edge = (self.spot == low) | (self.spot == self.count - 1 - low)
                total = jnp.where(edge, came, total)
        return total


def adam(moment, square, grad):
    moment_new = 0.9 * moment.astype(jnp.float32) + 0.1 * grad
    square_new = 0.95 * square.astype(jnp.float32) + 0.05 * grad * grad
    step = moment_new / correction_one / (jnp.sqrt(square_new / correction_two) + 1e-08)
    return step.astype(jnp.bfloat16)


def body(tokens, grad_out, routes, route_weights, swap_flags, weights, first_moment, second_moment):
    expert_count = lax.axis_size("expert")
    tok_count, route_count = routes.shape
    feat_width = tokens.shape[1]
    slot_cap = tok_count * route_count * 5 // (4 * expert_count)
    slot_total = tok_count * route_count
    slot_rows = expert_count * slot_cap
    positions = jnp.arange(expert_count, dtype=jnp.int32)
    paired = jnp.repeat(jnp.bitwise_and(swap_flags, 1), 2)
    traded = jnp.sum(jnp.where(positions == lax.axis_index("expert"), paired, 0)) == 1

    onehot = (routes.reshape(-1)[:, None] == positions[None, :]).astype(jnp.int32)
    slot_rank = jnp.sum((jnp.cumsum(onehot, axis=0) - onehot) * onehot, axis=1)
    slot_index = routes * slot_cap + slot_rank.reshape(tok_count, route_count)
    slots = jnp.arange(slot_rows, dtype=jnp.int32)
    pick = jnp.zeros((slot_rows, tok_count), jnp.float32)
    pick_weight = jnp.zeros((slot_rows, tok_count), jnp.float32)
    for r in range(route_count):
        hit = slots[:, None] == slot_index[:, r][None, :]
        pick = pick + jnp.where(hit, 1.0, 0.0)
        pick_weight = pick_weight + jnp.where(hit, route_weights[:, r][None, :], 0.0)
    pick = pick.astype(jnp.bfloat16)
    slot_weight = jnp.sum(pick_weight, axis=1)
    pick_weight = pick_weight.astype(jnp.bfloat16)

    def dispatch(rows):
        return lax.all_to_all(
            rows.reshape(expert_count, slot_cap, feat_width), "expert", 0, 0, tiled=True
        ).reshape(slot_rows, feat_width)

    send_tokens = jnp.dot(pick, tokens, preferred_element_type=jnp.float32).astype(jnp.bfloat16)
    token_slots = dispatch(send_tokens)
    send_grads = (
        slot_weight[:, None] * jnp.dot(pick, grad_out, preferred_element_type=jnp.float32)
    ).astype(jnp.bfloat16)
    grad_slots = dispatch(send_grads)

    hidden_width = weights.shape[2]
    gate_up_w, down_w = weights[0, 0:2], weights[0, 2]
    line = LineSum()
    gates, ups, hiddens = [], [], []

    def forward(c):
        rows = gate_up_w[:, c : c + PAIR].reshape(2 * PAIR, feat_width)
        both = line.add(contract_last(token_slots, rows).astype(jnp.bfloat16)).astype(jnp.float32)
        gate_pre, up_pre = both[:, :PAIR], both[:, PAIR:]
        gates.append(gate_pre)
        ups.append(up_pre)
        hiddens.append((gate_pre * jax.nn.sigmoid(gate_pre) * up_pre).astype(jnp.bfloat16))

    def settle(first, second, left, right):
        own = adam(first, second, contract_first(left, right))
        moved = lax.ppermute(own, "expert", [(i, i ^ 1) for i in range(expert_count)])
        return jnp.where(traded, moved, own)

    gate_up_steps, down_steps = [], []

    def backward(c):
        hidden_grad = line.add(
            contract_last(grad_slots, down_w[c : c + BLOCK]).astype(jnp.bfloat16)
        ).astype(jnp.float32)
        span = slice(c // PAIR, (c + BLOCK) // PAIR)
        gate_pre = jnp.concatenate(gates[span], axis=1)
        up_pre = jnp.concatenate(ups[span], axis=1)
        sig_gate = jax.nn.sigmoid(gate_pre)
        gate_grad = (hidden_grad * up_pre * sig_gate * (1.0 + gate_pre * (1.0 - sig_gate))).astype(
            jnp.bfloat16
        )
        up_grad = (hidden_grad * gate_pre * sig_gate).astype(jnp.bfloat16)
        own = (2 * BLOCK, feat_width)
        gate_up_steps.append(
            settle(
                first_moment[0, 0:2, c : c + BLOCK].reshape(own),
                second_moment[0, 0:2, c : c + BLOCK].reshape(own),
                jnp.concatenate([gate_grad, up_grad], axis=1),
                token_slots,
            ).reshape(2, BLOCK, feat_width)
        )

    def down(c):
        rows = slice(c, c + 2 * BLOCK)
        left = jnp.concatenate(hiddens[c // PAIR : (c + 2 * BLOCK) // PAIR], axis=1)
        down_steps.append(settle(first_moment[0, 2, rows], second_moment[0, 2, rows], left, grad_slots))

    blocks = list(range(0, hidden_width, BLOCK))
    pending = list(blocks)
    for number, c in enumerate(range(0, hidden_width, PAIR)):
        forward(c)
        if len(hiddens) * PAIR % (2 * BLOCK) == 0:
            down(len(hiddens) * PAIR - 2 * BLOCK)
        if number % 3 == 2 and len(pending) > len(blocks) // 2:
            backward(pending.pop(0))
    hidden = jnp.concatenate(hiddens, axis=1)
    output_slots = jnp.dot(
        hidden, down_w, preferred_element_type=jnp.float32
    ).astype(jnp.bfloat16)
    returned = dispatch(output_slots)
    combined = contract_first(pick_weight, returned).astype(jnp.bfloat16)
    for c in pending:
        backward(c)
    update = jnp.concatenate(
        [jnp.concatenate(gate_up_steps, axis=1), jnp.concatenate(down_steps, axis=0)[None]], axis=0
    )
    return combined, update[None]


def solution(mesh):
    placed = (
        P("expert", "tensor"),
        P("expert", "tensor"),
        P("expert", None),
        P("expert", None),
        P(),
        P("expert", None, None, "tensor"),
        P("expert", None, None, "tensor"),
        P("expert", None, None, "tensor"),
    )
    return jax.shard_map(
        body,
        mesh=mesh,
        in_specs=placed,
        out_specs=(P("expert", "tensor"), P("expert", None, None, "tensor")),
        check_vma=False,
    )
```
